512 devices in a mesh: brick: 64 (over x, z, core), relay: 8 (over y).
Axes of the slice: x: 4, y: 8, z: 8, core: 2. Of those that a mesh axis runs over, the one named last changes fastest.
Arguments:
- target: float32 [32, 512, 1536], P('relay', 'brick'), may hold values from 0.1 to 9, as said below
- frag_brick: int32 [32768, 1], P(('brick', 'relay')), may hold values from 0 to 63; in each aligned block of 64 rows (0 to 63, 64 to 127, ...) at most 2 rows name the same one
- bead_cell: int32 [32768, 128], P(('brick', 'relay')), may hold values from 0 to 49151
- bead_weight: bfloat16 [32768, 128], P(('brick', 'relay')), may hold values from 0.29882812 to 3
- bead_arm: float32 [3, 32768, 128], P(None, ('brick', 'relay')), may hold values from -12 to 12
- frag_angle: float32 [3, 32768], P(None, ('brick', 'relay')), may hold values from -3.140625 to 3.140625
Outputs:
- frag_grad: float32 [6, 32768], P(None, ('brick', 'relay'))
The draws below stay inside these ranges and needn't reach their ends.
Inputs may be any that keep to these rules, and one draw needn't show every extreme that they name: `frag_brick`: each device's 64 fragments name at most 2 fragments for one strip. `bead_cell`: A bead's voxel numbered (plane * 8 + x) * 1536 + y within the block of its fragment's strip on its owner's relay index. `target`: positive map intensity.
All inputs are finite; a program needn't handle non-finite values.
Results may differ from the reference program's by a relative error of at most 0.0003.
Values may be sent and summed in bfloat16 or wider, within the bound.
A program may use at most 128 MiB of HBM per device.

```python
import math
import jax
import jax.numpy as jnp
import numpy as np
from jax import lax

CX = 8
NY = 1536
CZ = 4
F_DEV = 64
BEADS = 128
KR = 4
MOST = 2
NX = 512
NZ = 32
FRAGS = 32768
N_BRICK = 64
N_RELAY = 8


def draw_target(key, part):
    shape = (NZ, NX, NY)
    across = jnp.arange(NX, dtype=jnp.float32)[None, :, None] / max(NX - 1, 1)
    profile = 1.0 + 2.0 * across
    rough = jax.random.uniform(key, shape, jnp.float32, 0.2, 1.8)
    return rough * profile


def plant(values, own_key, smallest, largest):
    place = [jax.random.randint(jax.random.fold_in(own_key, axis), (), 0, length) for axis, length in enumerate(values.shape)]
    widest = values.shape.index(max(values.shape))
    next_to = place[:widest] + [(place[widest] + 1) % values.shape[widest]] + place[widest + 1:]
    return values.at[tuple(place)].set(smallest).at[tuple(next_to)].set(largest)


def steps_of(rng, dims, cuts, smallest, high):
    def one(position, shards_of):
        draws = jax.random.uniform(jax.random.fold_in(jax.random.fold_in(rng, 6), position), (shards_of,), jnp.float32, smallest / len(cuts), high / len(cuts))
        return jnp.repeat(jnp.exp(draws), dims[position] // shards_of).reshape((-1,) + (1,) * (len(dims) - position - 1))

    gain = one(*cuts[0])
    for cut in cuts[1:]:
        gain = gain * one(*cut)
    return gain


def assign_block(stream_key, own, number, rows, amount, top, bound, skew):
    sequence = jax.random.permutation(stream_key, amount)
    heavy_load, ordinary = load_shares(amount, rows * top, bound, skew, True), load_shares(amount, rows * top, bound, skew, False)
    places = jnp.arange(amount)

    def named(tallies, offset_by):
        used = int((tallies > 0).sum())
        fixed = max(1, used // 4)
        moved = fixed + (places - fixed + offset_by * (used - fixed)) % max(1, amount - fixed)
        return jnp.zeros((amount,), jnp.int32).at[sequence[jnp.where(places < fixed, places, moved)]].set(jnp.asarray(tallies, jnp.int32))

    tallies = jnp.where(number % 4 == 0, named(heavy_load, number // 4), named(ordinary, number - number // 4 - 1))
    mixed = jax.random.permutation(jax.random.fold_in(own, 3), amount)
    source_of, sink = mixed[0:amount // 2 * 2:2], mixed[1:amount // 2 * 2:2]
    slack = jnp.minimum(tallies[source_of] - 1, bound - tallies[sink]) // 2
    slack = jnp.where((source_of == sequence[0]) | (sink == sequence[0]) | (tallies[sink] == 0), 0, jnp.maximum(slack, 0))
    moved = jax.random.randint(jax.random.fold_in(own, 4), (amount // 2,), 0, 1 << 20) % (slack + 1)
    tallies = tallies.at[source_of].add(-moved).at[sink].add(moved)
    members = jnp.searchsorted(jnp.cumsum(tallies), jnp.arange(rows * top), side="right").astype(jnp.int32)
    table = members.reshape(top, rows).T
    table = table[jax.random.permutation(jax.random.fold_in(own, 1), rows)]
    offset_by = jax.random.randint(jax.random.fold_in(own, 2), (rows, 1), 0, top)
    return jnp.take_along_axis(table, (jnp.arange(top)[None, :] + offset_by) % top, axis=1)


def load_shares(amount, total, bound, lean, full):
    portions = [(1 << 20) // math.isqrt(standing ** lean) + 1 for standing in range(1, amount + 1)]
    largest = bound if full else min(bound, max(-(-total // amount), total * portions[0] // sum(portions)))
    least = 1 if total - largest >= amount - 1 else 0
    counts, spare = [largest] + [least] * (amount - 1), total - largest - least * (amount - 1)
    while spare > 0:
        candidates = [i for i in range(1, amount) if counts[i] < largest] or [i for i in range(1, amount) if counts[i] < bound]
        whole, budget = sum([portions[i] for i in candidates]), spare
        for i in candidates:
            extra = min(bound - counts[i], max(1, budget * portions[i] // whole), spare)
            counts[i] = counts[i] + extra
            spare = spare - extra
    return np.array(counts)


def scatter_about(stream_key, dims, scale, limit, shards=(), held_as=jnp.bfloat16):
    values = jax.random.normal(stream_key, dims, jnp.float32) * scale
    if len(shards) > 0:
        values = steps_of(stream_key, dims, shards, -0.22, 0.18) * values
    return jnp.clip(values, min=-limit, max=limit).astype(held_as)


def setup_inputs(seed: int = 0) -> dict:
    key_list = jax.random.split(jax.random.key(seed), 7)
    target = draw_target(jax.random.fold_in(key_list[6], 71), 0)
    frag_brick_keys = jax.random.split(jax.random.fold_in(key_list[1], 1), FRAGS // F_DEV)
    frag_brick_turns = jax.random.permutation(jax.random.fold_in(key_list[1], 3), FRAGS // F_DEV)
    frag_brick = jax.vmap(lambda own, number: assign_block(jax.random.fold_in(key_list[1], 2), own, number, F_DEV, N_BRICK, 1, MOST, 2))(frag_brick_keys, frag_brick_turns).reshape((FRAGS, 1))
    bead_cell = plant(jax.random.randint(key_list[2], (FRAGS, BEADS), 0, CZ * CX * NY), jax.random.fold_in(key_list[2], 1), 0, (CZ * CX * NY) - 1).astype(jnp.int32)
    bead_weight = jnp.clip(jnp.exp(math.log(3.0) - 2.306499 * jax.random.uniform(key_list[3], (FRAGS, BEADS), jnp.float32) ** steps_of(key_list[3], (FRAGS, BEADS), ((0, 512),), -0.2, 0.2)), 0.29882812, 3.0).astype(jnp.bfloat16)
    bead_arm = scatter_about(key_list[4], (3, FRAGS, BEADS), 3.0, 12.0, ((1, 512),), jnp.float32)
    frag_angle = jnp.clip(jax.random.uniform(key_list[5], (3, FRAGS), jnp.float32, -3.140625, 3.140625), -3.140625, 3.140625)
    return dict(target=target, frag_brick=frag_brick, bead_cell=bead_cell, bead_weight=bead_weight, bead_arm=bead_arm, frag_angle=frag_angle)


SIGMA = 1.5
EPSILON = 1e-06

def kernel_values(half_width, derivative):
    offsets = np.arange(-half_width, half_width + 1) * 1.0
    gaussian = np.exp(-offsets ** 2 / (2.0 * SIGMA ** 2))
    gaussian = gaussian / gaussian.sum()
    if derivative:
        return -offsets / SIGMA ** 2 * gaussian
    return gaussian

def pass_taps(volume, along_dim, derivative):
    taps = kernel_values(KR, derivative)
    widths = [(KR, KR) if dim_id == along_dim else (0, 0) for dim_id in range(3)]
    widened = jnp.pad(volume, widths)
    out_len = volume.shape[along_dim]
    total = jnp.zeros(volume.shape, jnp.float32)
    for tap_id in range(2 * KR + 1):
        total = total + float(taps[2 * KR - tap_id]) * lax.slice_in_dim(widened, tap_id, tap_id + out_len, axis=along_dim)
    return total

def rotate_arms(angles, arms):
    cos_a, sin_a = (jnp.cos(angles[0]), jnp.sin(angles[0]))
    cos_b, sin_b = (jnp.cos(angles[1]), jnp.sin(angles[1]))
    cos_c, sin_c = (jnp.cos(angles[2]), jnp.sin(angles[2]))
    rot_rows = [[cos_a * cos_b, cos_a * sin_b * sin_c - sin_a * cos_c, cos_a * sin_b * cos_c + sin_a * sin_c], [sin_a * cos_b, sin_a * sin_b * sin_c + cos_a * cos_c, sin_a * sin_b * cos_c - cos_a * sin_c], [-sin_b, cos_b * sin_c, cos_b * cos_c]]
    return [sum((rot_rows[row_id][col_id][:, None] * arms[col_id] for col_id in range(3))) for row_id in range(3)]

def fragment_gradient(force, angles, arms):
    lever = rotate_arms(angles, arms)
    torque_x = lax.optimization_barrier(jnp.sum(lever[1] * force[2] - lever[2] * force[1], axis=1))
    torque_y = lax.optimization_barrier(jnp.sum(lever[2] * force[0] - lever[0] * force[2], axis=1))
    torque_z = lax.optimization_barrier(jnp.sum(lever[0] * force[1] - lever[1] * force[0], axis=1))
    return jnp.stack([lax.optimization_barrier(jnp.sum(force[0], axis=1)), lax.optimization_barrier(jnp.sum(force[1], axis=1)), lax.optimization_barrier(jnp.sum(force[2], axis=1)), torque_x, torque_y, torque_z])

def reference(target, frag_brick, bead_cell, bead_weight, bead_arm, frag_angle):
    frag_count = frag_brick.shape[0]
    layer = (jnp.arange(frag_count, dtype=jnp.int32) // F_DEV % N_RELAY).astype(jnp.int32)
    brick_of = frag_brick[:, 0].astype(jnp.int32)
    plane = layer[:, None] * CZ + bead_cell // (CX * NY)
    column = brick_of[:, None] * CX + bead_cell // NY % CX
    row_pos = bead_cell % NY
    flat_ids = ((plane * NX + column) * NY + row_pos).reshape(-1).astype(jnp.int32)
    weights = bead_weight.astype(jnp.float32)
    density = jnp.zeros((NZ * NX * NY,), jnp.float32).at[flat_ids].add(weights.reshape(-1)).reshape(NZ, NX, NY)
    model_map = pass_taps(pass_taps(pass_taps(density, 2, False), 1, False), 0, False)
    cross = jnp.sum(model_map * target)
    model_sq = jnp.sum(model_map * model_map)
    target_sq = jnp.sum(target * target)
    norm_model = jnp.sqrt(model_sq + EPSILON)
    norm_target = jnp.sqrt(target_sq + EPSILON)
    corr = cross / (norm_model * norm_target)
    scale = float(NX * NY * NZ)
    residual = scale * (target / (norm_model * norm_target) - corr * model_map / (norm_model * norm_model))
    along_z = pass_taps(residual, 0, False)
    slope_z = pass_taps(residual, 0, True)
    grad_x = pass_taps(pass_taps(along_z, 2, False), 1, True)
    grad_y = pass_taps(pass_taps(along_z, 2, True), 1, False)
    grad_z = pass_taps(pass_taps(slope_z, 2, False), 1, False)
    sampled = jnp.stack([grad_x.reshape(-1)[flat_ids], grad_y.reshape(-1)[flat_ids], grad_z.reshape(-1)[flat_ids]])
    force = sampled.reshape(3, frag_count, -1) * weights[None]
    return fragment_gradient(force, frag_angle, bead_arm)
```

```python
import functools

import jax
import jax.numpy as jnp
import numpy as np
from jax import lax
from jax.experimental import pallas as pl
from jax.experimental.pallas import tpu as pltpu
from jax.sharding import PartitionSpec as P

KR = 4
SIGMA = 1.5
EPSILON = 1e-06
WIDE = 256
F32 = jnp.float32
BF16 = jnp.bfloat16
MESH = pl.DeviceIdType.MESH


def kernel_values(half_width, derivative):
    offsets = np.arange(-half_width, half_width + 1) * 1.0
    gaussian = np.exp(-(offsets**2) / (2.0 * SIGMA**2))
    gaussian = gaussian / gaussian.sum()
    if derivative:
        return -offsets / SIGMA**2 * gaussian
    return gaussian


SMOOTH = [float(v) for v in kernel_values(KR, False)]
SLOPE = [float(v) for v in kernel_values(KR, True)]


def combine(behind, ahead, centre, which):
    if which == "g":
        total = SMOOTH[KR] * centre
        for t in range(1, KR + 1):
            total = total + SMOOTH[KR + t] * (behind[t - 1] + ahead[t - 1])
        return total
    total = SLOPE[KR + 1] * (behind[0] - ahead[0])
    for t in range(2, KR + 1):
        total = total + SLOPE[KR + t] * (behind[t - 1] - ahead[t - 1])
    return total


def blur_y(plane, which):
    rows, length = plane.shape
    wide = jnp.concatenate([plane, jnp.zeros((rows, 128), F32)], axis=1)
    behind = [pltpu.roll(wide, t, 1)[:, :length] for t in range(1, KR + 1)]
    ahead = [pltpu.roll(wide, length + 128 - t, 1)[:, :length] for t in range(1, KR + 1)]
    return combine(behind, ahead, plane, which)


def blur_x(left, own, right, kinds):
    cols = own.shape[0]
    row = lax.broadcasted_iota(jnp.int32, own.shape, 0)
    behind = [
        pltpu.roll(jnp.where(row >= cols - t, left, own), t, 0) for t in range(1, KR + 1)
    ]
    ahead = [
        pltpu.roll(jnp.where(row < t, right, own), cols - t, 0) for t in range(1, KR + 1)
    ]
    return [combine(behind, ahead, own, kind) for kind in kinds]


def blur_z(planes, kinds):
    own = len(planes) - 2 * KR
    done = []
    for kind in kinds:
        done.append(
            [
                combine(
                    [planes[KR + i - t] for t in range(1, KR + 1)],
                    [planes[KR + i + t] for t in range(1, KR + 1)],
                    planes[KR + i],
                    kind,
                )
                for i in range(own)
            ]
        )
    return done


def swap(plane):
    return pltpu.roll(plane, 4, 0)


def body(
    sizes,
    tgt,
    brick_of,
    cell,
    weight,
    arm,
    angle,
    out,
    bsend,
    brecv,
    lsend,
    lrecv,
    rsend,
    rrecv,
    tz,
    mz1,
    mz2,
    m1,
    mfull,
    tx_send,
    tx_recv,
    mx1_send,
    mx1_recv,
    mx2_send,
    mx2_recv,
    sc_send,
    sc_recv,
    density,
    code_ref,
    lhs_t,
    lhs_m,
    samp_t,
    samp_m,
    bead_s,
    bead_r,
    lev_s,
    lev_r,
    ret_s,
    ret_r,
    sc_s,
    sc_r,
    halo_s,
    halo_r,
):
    nb, nr, frags, beads, zn, xn, yn = sizes
    yc = yn // WIDE
    rows = zn * xn * yc
    me = lax.axis_index("brick")
    my = lax.axis_index("relay")
    b_up, b_down = lax.rem(me + 1, nb), lax.rem(me + nb - 1, nb)
    r_up, r_down = lax.rem(my + 1, nr), lax.rem(my + nr - 1, nr)
    has_left = jnp.where(me > 0, 1.0, 0.0).astype(F32)
    has_right = jnp.where(me < nb - 1, 1.0, 0.0).astype(F32)
    has_low = jnp.where(my > 0, 1.0, 0.0).astype(F32)
    has_high = jnp.where(my < nr - 1, 1.0, 0.0).astype(F32)

    barrier = pltpu.get_barrier_semaphore()

    def greet_brick(i, carry):
        pl.semaphore_signal(
            barrier, inc=1, device_id={"brick": lax.rem(me + i, nb)}, device_id_type=MESH
        )
        return carry

    def greet_relay(i, carry):
        pl.semaphore_signal(
            barrier, inc=1, device_id={"relay": lax.rem(my + i, nr)}, device_id_type=MESH
        )
        return carry

    lax.fori_loop(1, nb, greet_brick, 0)
    lax.fori_loop(1, nr, greet_relay, 0)

    row_f = lax.broadcasted_iota(jnp.int32, (frags, frags), 0)
    col_f = lax.broadcasted_iota(jnp.int32, (frags, frags), 1)
    brick_col = brick_of[...].astype(F32)
    brick_row = jnp.sum(jnp.where(row_f == col_f, brick_col, 0.0), axis=0, keepdims=True)
    twin = jnp.where((brick_col == brick_row) & (row_f < col_f), 1.0, 0.0)
    rank_row = jnp.sum(twin, axis=0, keepdims=True)
    brick_iota = lax.broadcasted_iota(jnp.int32, (nb, frags), 0).astype(F32)
    goes = jnp.where(brick_iota == brick_row, 1.0, 0.0)
    first = jnp.where(rank_row < 0.5, 1.0, 0.0)
    pick = [goes * first, goes * (1.0 - first)]
    picks = jnp.concatenate(pick, axis=0)

    cells = cell[...].astype(F32)
    line = jnp.floor((cells + 0.5) * (1.0 / yn))
    y_pos = cells - line * yn
    chunk = jnp.floor((y_pos + 0.5) * (1.0 / WIDE))
    column = y_pos - chunk * WIDE
    row_id = chunk * (zn * xn) + line
    w = weight[...]
    w32 = w.astype(F32)
    early = jnp.concatenate([row_id.astype(BF16), column.astype(BF16), w], axis=1)
    sent = jnp.dot(picks.astype(BF16), early, preferred_element_type=F32)
    packed = (
        sent[:, 2 * beads :] * 512.0
    ).astype(jnp.int32) * 65536 + (sent[:, :beads] * WIDE + sent[:, beads : 2 * beads]).astype(
        jnp.int32
    )
    code_ref[...] = packed

    def lay_out(p, carry):
        for k in range(2):
            bsend[p, pl.ds(k, 1), :] = code_ref[pl.ds(k * nb + p, 1), :]
        return carry

    lax.fori_loop(0, nb, lay_out, 0)

    pl.semaphore_wait(barrier, nb + nr - 2)

    def bead_copy(far, slot):
        return pltpu.make_async_remote_copy(
            src_ref=bsend.at[far],
            dst_ref=brecv.at[slot],
            send_sem=bead_s.at[far],
            recv_sem=bead_r.at[slot],
            device_id={"brick": far},
            device_id_type=MESH,
        )

    def lever_copy(far, slot):
        return pltpu.make_async_remote_copy(
            src_ref=lsend.at[pl.ds(pl.multiple_of(far * 8, 8), 8)],
            dst_ref=lrecv.at[pl.ds(pl.multiple_of(slot * 8, 8), 8)],
            send_sem=lev_s.at[far],
            recv_sem=lev_r.at[slot],
            device_id={"brick": far},
            device_id_type=MESH,
        )

    def return_copy(far, slot):
        return pltpu.make_async_remote_copy(
            src_ref=rsend.at[far],
            dst_ref=rrecv.at[slot],
            send_sem=ret_s.at[far],
            recv_sem=ret_r.at[slot],
            device_id={"brick": far},
            device_id_type=MESH,
        )

    def scalar_copy(far, slot):
        return pltpu.make_async_remote_copy(
            src_ref=sc_send,
            dst_ref=sc_recv.at[slot],
            send_sem=sc_s.at[far],
            recv_sem=sc_r.at[slot],
            device_id={"relay": far},
            device_id_type=MESH,
        )

    def start_all(copy, size, mine):
        def one(i, carry):
            copy(lax.rem(mine + i, size), mine).start()
            return carry

        lax.fori_loop(1, size, one, 0)

    def wait_all(copy, size, mine, sending):
        def one(i, carry):
            far = lax.rem(mine + i, size)
            if sending:
                copy(far, mine).wait_send()
            else:
                copy(far, far).wait_recv()
            return carry

        lax.fori_loop(1, size, one, 0)

    def halo(src, dst, number, where):
        return pltpu.make_async_remote_copy(
            src_ref=src,
            dst_ref=dst,
            send_sem=halo_s.at[number],
            recv_sem=halo_r.at[number],
            device_id=where,
            device_id_type=MESH,
        )

    t_z = [
        halo(tgt, tz.at[0], 0, {"relay": r_up}),
        halo(tgt, tz.at[1], 1, {"relay": r_down}),
    ]
    t_x = [
        halo(tx_send.at[0], tx_recv.at[0], 2, {"brick": b_up}),
        halo(tx_send.at[1], tx_recv.at[1], 3, {"brick": b_down}),
    ]
    m_x1 = [
        halo(mx1_send.at[0], mx1_recv.at[0], 4, {"brick": b_up}),
        halo(mx1_send.at[1], mx1_recv.at[1], 5, {"brick": b_down}),
    ]
    m_z1 = [
        halo(m1, mz1.at[0], 6, {"relay": r_up}),
        halo(m1, mz1.at[1], 7, {"relay": r_down}),
    ]
    m_z2 = [
        halo(mfull, mz2.at[0], 8, {"relay": r_up}),
        halo(mfull, mz2.at[1], 9, {"relay": r_down}),
    ]
    m_x2 = [
        halo(mx2_send.at[0], mx2_recv.at[0], 10, {"brick": b_up}),
        halo(mx2_send.at[1], mx2_recv.at[1], 11, {"brick": b_down}),
    ]

    def start(pair):
        for copy in pair:
            copy.start()

    def wait_recv(pair):
        for copy in pair:
            copy.wait_recv()

    def z_planes(own, got):
        return (
            [got[0, i] * has_low for i in range(zn)]
            + own
            + [got[1, i] * has_high for i in range(zn)]
        )

    def pack_x(send, pairs):
        row = lax.broadcasted_iota(jnp.int32, (xn, yn), 0)
        for i, (one, two) in enumerate(pairs):
            send[0, i] = jnp.where(row < 4, swap(one), two)
            send[1, i] = jnp.where(row < 4, one, swap(two))

    def unpack_x(got, i):
        from_left, from_right = got[0, i] * has_left, got[1, i] * has_right
        return (swap(from_left), from_right), (from_left, swap(from_right))

    start_all(bead_copy, nb, me)
    start(t_z)
    brecv[me] = bsend[me]

    cos_sin = []
    for j in range(3):
        turn = angle[pl.ds(j, 1), :]
        pair = []
        for fn in (jnp.cos, jnp.sin):
            pair.append(
                jnp.sum(jnp.where(row_f == col_f, fn(turn), 0.0), axis=1, keepdims=True)
            )
        cos_sin.append(pair)
    (cos_a, sin_a), (cos_b, sin_b), (cos_c, sin_c) = cos_sin
    rot = [
        [
            cos_a * cos_b,
            cos_a * sin_b * sin_c - sin_a * cos_c,
            cos_a * sin_b * cos_c + sin_a * sin_c,
        ],
        [
            sin_a * cos_b,
            sin_a * sin_b * sin_c + cos_a * cos_c,
            sin_a * sin_b * cos_c - cos_a * sin_c,
        ],
        [-sin_b, cos_b * sin_c, cos_b * cos_c],
    ]
    arms = [arm[j] for j in range(3)]
    late = [w32]
    for j in range(3):
        late.append(w32 * (rot[j][0] * arms[0] + rot[j][1] * arms[1] + rot[j][2] * arms[2]))
    late = jnp.concatenate(late, axis=1)
    moved = jnp.dot(
        picks, late, precision=lax.Precision.HIGHEST, preferred_element_type=F32
    )
    for k in range(2):
        for j in range(4):
            lsend[pl.ds(k * 4 + j, nb, stride=8), :] = moved[
                k * nb : (k + 1) * nb, j * beads : (j + 1) * beads
            ]
    start_all(lever_copy, nb, me)
    mine8 = pl.ds(pl.multiple_of(me * 8, 8), 8)
    lrecv[mine8, :] = lsend[mine8, :]

    t_own = [tgt[i] for i in range(zn)]
    t_sq = jnp.zeros((), F32)
    for plane in t_own:
        t_sq = t_sq + jnp.sum(plane * plane)
    wait_recv(t_z)
    t_g, t_d = blur_z(z_planes(t_own, tz), ("g", "d"))
    pack_x(tx_send, list(zip(t_g, t_d)))
    start(t_x)

    wait_all(bead_copy, nb, me, False)
    step = 4
    row_iota = lax.broadcasted_iota(jnp.int32, (rows, 2 * beads * step), 0)
    col_iota = lax.broadcasted_iota(jnp.int32, (WIDE, 2 * beads * step), 0)
    density[...] = jnp.zeros_like(density)

    def splat(i, carry):
        pieces = []
        for j in range(step):
            two = brecv[i * step + j]
            pieces += [two[0:1], two[1:2]]
        word = jnp.concatenate(pieces, axis=1)
        code = lax.bitwise_and(word, 65535)
        mass = lax.shift_right_logical(word, 16).astype(F32) * (1.0 / 512.0)
        at_row = lax.shift_right_logical(code, 8)
        at_col = lax.bitwise_and(code, WIDE - 1)
        lhs = jnp.where(row_iota == at_row, 1.0, 0.0).astype(BF16)
        rhs = jnp.where(col_iota == at_col, mass, 0.0).astype(BF16)
        density[...] += lax.dot_general(
            lhs, rhs, (((1,), (1,)), ((), ())), preferred_element_type=F32
        )
        return carry

    lax.fori_loop(0, nb // step, splat, 0)

    def plane_of(z):
        return jnp.concatenate(
            [density[(c * zn + z) * xn : (c * zn + z + 1) * xn, :] for c in range(yc)], axis=1
        )

    d_own = [blur_y(plane_of(z), "g") for z in range(zn)]
    pack_x(mx1_send, [(d_own[2 * i], d_own[2 * i + 1]) for i in range(zn // 2)])
    start(m_x1)

    def fields(z_g, z_d, got, lhs):
        parts = [[], [], []]
        for i in range(zn):
            (left_g, right_g), (left_d, right_d) = unpack_x(got, i)
            gg, slope = blur_x(left_g, z_g[i], right_g, ("g", "d"))
            (gd,) = blur_x(left_d, z_d[i], right_d, ("g",))
            parts[0].append(blur_y(slope, "g"))
            parts[1].append(blur_y(gg, "d"))
            parts[2].append(blur_y(gd, "g"))
        for f in range(3):
            stacked = jnp.concatenate(
                [
                    parts[f][z][:, c * WIDE : (c + 1) * WIDE]
                    for c in range(yc)
                    for z in range(zn)
                ],
                axis=0,
            )
            high = stacked.astype(BF16)
            low = (stacked - high.astype(F32)).astype(BF16)
            lhs[pl.ds(f * rows, rows), 0:WIDE] = high
            lhs[pl.ds(f * rows, rows), WIDE : 2 * WIDE] = low

    srow_iota = lax.broadcasted_iota(jnp.int32, (rows, 2 * beads), 0)
    scol_iota = lax.broadcasted_iota(jnp.int32, (WIDE, 2 * beads), 0)

    def sample(lhs, samp, begin, end):
        def one(p, carry):
            two = brecv[p]
            code = lax.bitwise_and(jnp.concatenate([two[0:1], two[1:2]], axis=1), 65535)
            at_row = lax.shift_right_logical(code, 8)
            at_col = lax.bitwise_and(code, WIDE - 1)
            hot = jnp.where(scol_iota == at_col, 1.0, 0.0).astype(BF16)
            found = jnp.dot(
                lhs[...], jnp.concatenate([hot, hot], axis=0), preferred_element_type=F32
            )
            here = srow_iota == at_row
            for f in range(3):
                value = jnp.sum(
                    jnp.where(here, found[f * rows : (f + 1) * rows], 0.0),
                    axis=0,
                    keepdims=True,
                )
                for k in range(2):
                    samp[f * 2 + k, pl.ds(p, 1), :] = value[:, k * beads : (k + 1) * beads]
            return carry

        lax.fori_loop(begin, end, one, 0)

    wait_recv(t_x)
    fields(t_g, t_d, tx_recv, lhs_t)

    wait_recv(m_x1)
    for i in range(zn // 2):
        halves = unpack_x(mx1_recv, i)
        for j in range(2):
            left, right = halves[j]
            (m1[2 * i + j],) = blur_x(left, d_own[2 * i + j], right, ("g",))
    start(m_z1)

    sample(lhs_t, samp_t, 0, nb // 2)

    wait_recv(m_z1)
    (m_own,) = blur_z(z_planes([m1[i] for i in range(zn)], mz1), ("g",))
    for i in range(zn):
        mfull[i] = m_own[i]
    start(m_z2)

    cross, m_sq = jnp.zeros((), F32), jnp.zeros((), F32)
    for i in range(zn):
        cross = cross + jnp.sum(m_own[i] * tgt[i])
        m_sq = m_sq + jnp.sum(m_own[i] * m_own[i])
    lane8 = lax.broadcasted_iota(jnp.int32, (8, 128), 1)
    sc_send[...] = jnp.where(
        lane8 == 0, cross, jnp.where(lane8 == 1, m_sq, jnp.where(lane8 == 2, t_sq, 0.0))
    )
    sc_recv[my] = sc_send[...]
    start_all(scalar_copy, nr, my)

    sample(lhs_t, samp_t, nb // 2, nb)

    wait_recv(m_z2)
    m_g, m_d = blur_z(z_planes([mfull[i] for i in range(zn)], mz2), ("g", "d"))
    pack_x(mx2_send, list(zip(m_g, m_d)))
    start(m_x2)

    wait_all(lever_copy, nb, me, False)
    lane = lax.broadcasted_iota(jnp.int32, (nb, 128), 1)

    def sums_into(total, samp, base):
        for k in range(2):
            mass, ux, uy, uz = [lrecv[pl.ds(k * 4 + j, nb, stride=8), :] for j in range(4)]
            gx, gy, gz = [samp[f * 2 + k] for f in range(3)]
            six = (
                mass * gx,
                mass * gy,
                mass * gz,
                uy * gz - uz * gy,
                uz * gx - ux * gz,
                ux * gy - uy * gx,
            )
            for j, term in enumerate(six):
                total = jnp.where(
                    lane == base + k * 6 + j, jnp.sum(term, axis=1, keepdims=True), total
                )
        return total

    total = sums_into(jnp.zeros((nb, 128), F32), samp_t, 0)

    wait_recv(m_x2)
    fields(m_g, m_d, mx2_recv, lhs_m)
    sample(lhs_m, samp_m, 0, nb)
    total = sums_into(total, samp_m, 12)

    wait_all(scalar_copy, nr, my, False)
    shared = sc_recv[0]
    for i in range(1, nr):
        shared = shared + sc_recv[i]
    for j in range(3):
        total = jnp.where(lane == 24 + j, shared[0:1, j : j + 1], total)
    code_total = total
    samp_t[0] = code_total

    def lay_return(p, carry):
        rsend[p] = samp_t[0, pl.ds(p, 1), :]
        return carry

    lax.fori_loop(0, nb, lay_return, 0)
    start_all(return_copy, nb, me)
    rrecv[me] = rsend[me]

    for pair in (t_z, t_x, m_x1, m_z1, m_z2, m_x2):
        for copy in pair:
            copy.wait_send()
    wait_all(bead_copy, nb, me, True)
    wait_all(lever_copy, nb, me, True)
    wait_all(scalar_copy, nr, my, True)
    wait_all(return_copy, nb, me, False)

    def lay_got(p, carry):
        samp_t[1, pl.ds(p, 1), :] = rrecv[p]
        return carry

    lax.fori_loop(0, nb, lay_got, 0)
    got = samp_t[1]
    sums = jnp.sum(got[:, 24:27], axis=0, keepdims=True)
    cross, m_sq, t_sq = sums[:, 0:1], sums[:, 1:2], sums[:, 2:3]
    norm_m = jnp.sqrt(m_sq + EPSILON)
    norm_t = jnp.sqrt(t_sq + EPSILON)
    corr = cross / (norm_m * norm_t)
    voxels = float(nb * xn * nr * zn * yn)
    of_target = voxels / (norm_m * norm_t)
    of_model = voxels * corr / (norm_m * norm_m)
    for j in range(6):
        value = jnp.zeros((1, frags), F32)
        for k in range(2):
            from_t = jnp.sum(pick[k] * got[:, k * 6 + j : k * 6 + j + 1], axis=0, keepdims=True)
            at_m = 12 + k * 6 + j
            from_m = jnp.sum(pick[k] * got[:, at_m : at_m + 1], axis=0, keepdims=True)
            value = value + (of_target * from_t - of_model * from_m)
        out[pl.ds(j, 1), :] = value
    wait_all(return_copy, nb, me, True)


def shards(target, frag_brick, bead_cell, bead_weight, bead_arm, frag_angle):
    nb, nr = lax.axis_size("brick"), lax.axis_size("relay")
    frags, beads = bead_cell.shape
    zn, xn, yn = target.shape
    rows = zn * xn * (yn // WIDE)
    sizes = (nb, nr, frags, beads, zn, xn, yn)
    vmem = pltpu.VMEM
    block = (zn, xn, yn)
    dma = pltpu.SemaphoreType.DMA
    scratch = [
        vmem((nb, 2, beads), jnp.int32),
        vmem((nb, 2, beads), jnp.int32),
        vmem((nb * 8, beads), F32),
        vmem((nb * 8, beads), F32),
        vmem((nb, 1, 128), F32),
        vmem((nb, 1, 128), F32),
        vmem((2,) + block, F32),
        vmem((2,) + block, F32),
        vmem((2,) + block, F32),
        vmem(block, F32),
        vmem(block, F32),
        vmem((2,) + block, F32),
        vmem((2,) + block, F32),
        vmem((2, zn // 2, xn, yn), F32),
        vmem((2, zn // 2, xn, yn), F32),
        vmem((2,) + block, F32),
        vmem((2,) + block, F32),
        vmem((8, 128), F32),
        vmem((nr, 8, 128), F32),
        vmem((rows, WIDE), F32),
        vmem((2 * nb, beads), jnp.int32),
        vmem((3 * rows, 2 * WIDE), BF16),
        vmem((3 * rows, 2 * WIDE), BF16),
        vmem((6, nb, beads), F32),
        vmem((6, nb, beads), F32),
        dma((nb,)),
        dma((nb,)),
        dma((nb,)),
        dma((nb,)),
        dma((nb,)),
        dma((nb,)),
        dma((nr,)),
        dma((nr,)),
        dma((12,)),
        dma((12,)),
    ]
    here = pl.BlockSpec(memory_space=pltpu.VMEM)
    return pl.pallas_call(
        functools.partial(body, sizes),
        out_shape=jax.ShapeDtypeStruct((6, frags), F32),
        in_specs=[here] * 6,
        out_specs=here,
        scratch_shapes=scratch,
        compiler_params=pltpu.CompilerParams(
            collective_id=0, has_side_effects=True, vmem_limit_bytes=56 * 1024 * 1024
        ),
    )(target, frag_brick, bead_cell, bead_weight, bead_arm, frag_angle)


def solution(mesh):
    placed = (
        P("relay", "brick", None),
        P(("brick", "relay"), None),
        P(("brick", "relay"), None),
        P(("brick", "relay"), None),
        P(None, ("brick", "relay"), None),
        P(None, ("brick", "relay")),
    )
    return jax.shard_map(
        shards, mesh=mesh, in_specs=placed, out_specs=P(None, ("brick", "relay")), check_vma=False
    )
```

```python
import functools

import jax
import jax.numpy as jnp
import numpy as np
from jax import lax
from jax.experimental import pallas as pl
from jax.experimental.pallas import tpu as pltpu
from jax.sharding import PartitionSpec as P

KR = 4
SIGMA = 1.5
EPSILON = 1e-06
WIDE = 256
F32 = jnp.float32
BF16 = jnp.bfloat16
MESH = pl.DeviceIdType.MESH


def kernel_values(half_width, derivative):
    offsets = np.arange(-half_width, half_width + 1) * 1.0
    gaussian = np.exp(-(offsets**2) / (2.0 * SIGMA**2))
    gaussian = gaussian / gaussian.sum()
    if derivative:
        return -offsets / SIGMA**2 * gaussian
    return gaussian


SMOOTH = [float(v) for v in kernel_values(KR, False)]
SLOPE = [float(v) for v in kernel_values(KR, True)]


def combine(behind, ahead, centre, which):
    if which == "g":
        total = SMOOTH[KR] * centre
        for t in range(1, KR + 1):
            total = total + SMOOTH[KR + t] * (behind[t - 1] + ahead[t - 1])
        return total
    total = SLOPE[KR + 1] * (behind[0] - ahead[0])
    for t in range(2, KR + 1):
        total = total + SLOPE[KR + t] * (behind[t - 1] - ahead[t - 1])
    return total


def blur_y(plane, which):
    rows, length = plane.shape
    wide = jnp.concatenate([plane, jnp.zeros((rows, 128), F32)], axis=1)
    behind = [pltpu.roll(wide, t, 1)[:, :length] for t in range(1, KR + 1)]
    ahead = [pltpu.roll(wide, length + 128 - t, 1)[:, :length] for t in range(1, KR + 1)]
    return combine(behind, ahead, plane, which)


def blur_x(left, own, right, kinds):
    cols = own.shape[0]
    row = lax.broadcasted_iota(jnp.int32, own.shape, 0)
    behind = [
        pltpu.roll(jnp.where(row >= cols - t, left, own), t, 0) for t in range(1, KR + 1)
    ]
    ahead = [
        pltpu.roll(jnp.where(row < t, right, own), cols - t, 0) for t in range(1, KR + 1)
    ]
    return [combine(behind, ahead, own, kind) for kind in kinds]


def blur_z(planes, kinds):
    own = len(planes) - 2 * KR
    done = []
    for kind in kinds:
        done.append(
            [
                combine(
                    [planes[KR + i - t] for t in range(1, KR + 1)],
                    [planes[KR + i + t] for t in range(1, KR + 1)],
                    planes[KR + i],
                    kind,
                )
                for i in range(own)
            ]
        )
    return done


def swap(plane):
    return pltpu.roll(plane, 4, 0)


def ring_near(j):
    return j + j // 2 - 2 * (j // 3)


def total_of(value):
    return jnp.sum(jnp.sum(value, axis=1, keepdims=True), axis=0, keepdims=True)


def body(
    sizes,
    tgt_in,
    brick_in,
    cell_in,
    weight_in,
    arm_in,
    angle_in,
    out,
    tgt,
    brick_of,
    cell,
    weight,
    arm,
    angle,
    bsend,
    brecv,
    lsend,
    lrecv,
    rsend,
    rrecv,
    fin,
    tz,
    mz1,
    mz2,
    m1,
    mfull,
    tx_send,
    tx_recv,
    mx1_send,
    mx1_recv,
    mx2_send,
    mx2_recv,
    s1_send,
    s1_recv,
    s2_send,
    s2_recv,
    density,
    lhs,
    load,
    bead_s,
    bead_r,
    lev_s,
    lev_r,
    ret_s,
    ret_r,
    sum_s,
    sum_r,
    halo_s,
    halo_r,
):
    nb, nr, frags, beads, zn, xn, yn = sizes
    yc = yn // WIDE
    rows = zn * xn * yc
    slots = 2 * nb
    crowds = nb // 8
    wide_x = crowds // 2
    me = lax.axis_index("brick")
    my = lax.axis_index("relay")
    my_crowd = me // 8
    my_x, my_half = my_crowd // 2, my_crowd % 2
    b_up, b_down = lax.rem(me + 1, nb), lax.rem(me + nb - 1, nb)
    r_up, r_down = lax.rem(my + 1, nr), lax.rem(my + nr - 1, nr)
    has_left = jnp.where(me > 0, 1.0, 0.0).astype(F32)
    has_right = jnp.where(me < nb - 1, 1.0, 0.0).astype(F32)
    has_low = jnp.where(my > 0, 1.0, 0.0).astype(F32)
    has_high = jnp.where(my < nr - 1, 1.0, 0.0).astype(F32)

    barrier = pltpu.get_barrier_semaphore()

    def greet_brick(i, carry):
        pl.semaphore_signal(
            barrier, inc=1, device_id={"brick": lax.rem(me + i, nb)}, device_id_type=MESH
        )
        return carry

    def greet_relay(i, carry):
        pl.semaphore_signal(
            barrier, inc=1, device_id={"relay": lax.rem(my + i, nr)}, device_id_type=MESH
        )
        return carry

    lax.fori_loop(1, nb, greet_brick, 0)
    lax.fori_loop(1, nr, greet_relay, 0)
    loads = [
        pltpu.make_async_copy(src, dst, load.at[i])
        for i, (src, dst) in enumerate(
            (
                (brick_in, brick_of),
                (cell_in, cell),
                (weight_in, weight),
                (arm_in, arm),
                (angle_in, angle),
                (tgt_in, tgt),
            )
        )
    ]
    for copy in loads:
        copy.start()
    for copy in loads:
        copy.wait()

    row_f = lax.broadcasted_iota(jnp.int32, (frags, frags), 0)
    col_f = lax.broadcasted_iota(jnp.int32, (frags, frags), 1)
    brick_row = brick_of[...].astype(F32)
    brick_col = jnp.sum(jnp.where(row_f == col_f, brick_row, 0.0), axis=1, keepdims=True)
    twin = jnp.where((brick_col == brick_row) & (row_f < col_f), 1.0, 0.0)
    rank_row = jnp.minimum(jnp.sum(twin, axis=0, keepdims=True), 1.0)
    slot_iota = lax.broadcasted_iota(jnp.int32, (slots, frags), 0).astype(F32)
    picks = jnp.where(slot_iota == brick_row * 2.0 + rank_row, 1.0, 0.0)

    cells = cell[...].astype(F32)
    line = jnp.floor((cells + 0.5) * (1.0 / yn))
    y_pos = cells - line * yn
    chunk = jnp.floor((y_pos + 0.5) * (1.0 / WIDE))
    column = y_pos - chunk * WIDE
    row_id = chunk * (zn * xn) + line
    w = weight[...]
    w32 = w.astype(F32)
    early = jnp.concatenate([row_id.astype(BF16), column.astype(BF16), w], axis=1)
    sent = jnp.dot(picks.astype(BF16), early, preferred_element_type=F32)
    code = (sent[:, :beads] * WIDE + sent[:, beads : 2 * beads]).astype(jnp.int32)
    packed = (sent[:, 2 * beads :] * 512.0).astype(jnp.int32) * 65536 + code
    for p in range(nb):
        bsend[p] = packed[2 * p : 2 * p + 2]

    cos_sin = []
    for j in range(3):
        turn = angle[pl.ds(j, 1), :]
        pair = []
        for fn in (jnp.cos, jnp.sin):
            pair.append(
                jnp.sum(jnp.where(row_f == col_f, fn(turn), 0.0), axis=1, keepdims=True)
            )
        cos_sin.append(pair)
    (cos_a, sin_a), (cos_b, sin_b), (cos_c, sin_c) = cos_sin
    rot = [
        [
            cos_a * cos_b,
            cos_a * sin_b * sin_c - sin_a * cos_c,
            cos_a * sin_b * cos_c + sin_a * sin_c,
        ],
        [
            sin_a * cos_b,
            sin_a * sin_b * sin_c + cos_a * cos_c,
            sin_a * sin_b * cos_c - cos_a * sin_c,
        ],
        [-sin_b, cos_b * sin_c, cos_b * cos_c],
    ]
    arms = [arm[j] for j in range(3)]
    late = [w32]
    for j in range(3):
        late.append(w32 * (rot[j][0] * arms[0] + rot[j][1] * arms[1] + rot[j][2] * arms[2]))
    late = jnp.concatenate(late, axis=1)
    moved = jnp.dot(
        picks, late, precision=lax.Precision.HIGHEST, preferred_element_type=F32
    )
    for j in range(4):
        lsend[pl.ds(j, slots, stride=4), :] = moved[:, j * beads : (j + 1) * beads]

    pl.semaphore_wait(barrier, nb + nr - 2)

    def bead_copy(far):
        return pltpu.make_async_remote_copy(
            src_ref=bsend.at[far],
            dst_ref=brecv.at[me],
            send_sem=bead_s,
            recv_sem=bead_r.at[my_crowd],
            device_id={"brick": far},
            device_id_type=MESH,
        )

    def lever_copy(far):
        return pltpu.make_async_remote_copy(
            src_ref=lsend.at[pl.ds(pl.multiple_of(far * 8, 8), 8)],
            dst_ref=lrecv.at[pl.ds(pl.multiple_of(me * 8, 8), 8)],
            send_sem=lev_s,
            recv_sem=lev_r,
            device_id={"brick": far},
            device_id_type=MESH,
        )

    def return_copy(far):
        return pltpu.make_async_remote_copy(
            src_ref=rsend.at[far],
            dst_ref=rrecv.at[me],
            send_sem=ret_s,
            recv_sem=ret_r.at[my_crowd],
            device_id={"brick": far},
            device_id_type=MESH,
        )

    def brick_sum_copy(far):
        return pltpu.make_async_remote_copy(
            src_ref=s1_send,
            dst_ref=s1_recv.at[me],
            send_sem=sum_s.at[0],
            recv_sem=sum_r.at[0],
            device_id={"brick": far},
            device_id_type=MESH,
        )

    def relay_sum_copy(far):
        return pltpu.make_async_remote_copy(
            src_ref=s2_send,
            dst_ref=s2_recv.at[my],
            send_sem=sum_s.at[1],
            recv_sem=sum_r.at[1],
            device_id={"relay": far},
            device_id_type=MESH,
        )

    def bytes_in(ref, sem, where):
        pltpu.make_async_remote_copy(
            src_ref=ref,
            dst_ref=ref,
            send_sem=sem,
            recv_sem=sem,
            device_id=where,
            device_id_type=MESH,
        ).wait_recv()

    def bytes_out(ref, sem, where):
        pltpu.make_async_remote_copy(
            src_ref=ref,
            dst_ref=ref,
            send_sem=sem,
            recv_sem=sem,
            device_id=where,
            device_id_type=MESH,
        ).wait_send()

    beside = {"brick": b_up}

    def near_crowd(i):
        return lax.rem(my_x + ring_near(i // 2), wide_x) * 2 + lax.rem(my_half + i % 2, 2)

    def start_crowd(copy, crowd):
        for j in range(8):
            copy(crowd * 8 + j).start()

    def start_own(copy):
        for j in range(1, 8):
            copy(my_crowd * 8 + lax.rem(me + j, 8)).start()

    def start_bricks(copy):
        def one(i, carry):
            start_crowd(copy, near_crowd(crowds - 1 - i))
            return carry

        lax.fori_loop(0, crowds - 1, one, 0)
        start_own(copy)

    def halo(src, dst, number, where):
        return pltpu.make_async_remote_copy(
            src_ref=src,
            dst_ref=dst,
            send_sem=halo_s.at[number],
            recv_sem=halo_r.at[number],
            device_id=where,
            device_id_type=MESH,
        )

    t_z = [
        halo(tgt, tz.at[0], 0, {"relay": r_up}),
        halo(tgt, tz.at[1], 1, {"relay": r_down}),
    ]
    t_x = [
        halo(tx_send.at[0], tx_recv.at[0], 2, {"brick": b_up}),
        halo(tx_send.at[1], tx_recv.at[1], 3, {"brick": b_down}),
    ]
    m_x1 = [
        halo(mx1_send.at[0], mx1_recv.at[0], 4, {"brick": b_up}),
        halo(mx1_send.at[1], mx1_recv.at[1], 5, {"brick": b_down}),
    ]
    m_z1 = [
        halo(m1, mz1.at[0], 6, {"relay": r_up}),
        halo(m1, mz1.at[1], 7, {"relay": r_down}),
    ]
    m_z2 = [
        halo(mfull, mz2.at[0], 8, {"relay": r_up}),
        halo(mfull, mz2.at[1], 9, {"relay": r_down}),
    ]
    m_x2 = [
        halo(mx2_send.at[0], mx2_recv.at[0], 10, {"brick": b_up}),
        halo(mx2_send.at[1], mx2_recv.at[1], 11, {"brick": b_down}),
    ]

    def start(pair):
        for copy in pair:
            copy.start()

    def wait_recv(pair):
        for copy in pair:
            copy.wait_recv()

    def z_planes(own, got):
        return (
            [got[0, i] * has_low for i in range(zn)]
            + own
            + [got[1, i] * has_high for i in range(zn)]
        )

    def pack_x(send, pairs):
        row = lax.broadcasted_iota(jnp.int32, (xn, yn), 0)
        for i, (one, two) in enumerate(pairs):
            send[0, i] = jnp.where(row < 4, swap(one), two)
            send[1, i] = jnp.where(row < 4, one, swap(two))

    def unpack_x(from_left, from_right):
        from_left, from_right = from_left * has_left, from_right * has_right
        return (swap(from_left), from_right), (from_left, swap(from_right))

    start_bricks(bead_copy)
    start(t_z)
    start_bricks(lever_copy)
    brecv[me] = bsend[me]
    mine8 = pl.ds(pl.multiple_of(me * 8, 8), 8)
    lrecv[mine8, :] = lsend[mine8, :]

    row_iota = lax.broadcasted_iota(jnp.int32, (rows, 16 * beads), 0)
    col_iota = lax.broadcasted_iota(jnp.int32, (WIDE, 16 * beads), 0)
    density[...] = jnp.zeros_like(density)

    def splat(crowd):
        pieces = []
        for j in range(8):
            two = brecv[crowd * 8 + j]
            pieces += [two[0:1], two[1:2]]
        word = jnp.concatenate(pieces, axis=1)
        code = lax.bitwise_and(word, 65535)
        mass = lax.shift_right_logical(word, 16).astype(F32) * (1.0 / 512.0)
        at_row = lax.shift_right_logical(code, 8)
        at_col = lax.bitwise_and(code, WIDE - 1)
        left = jnp.where(row_iota == at_row, 1.0, 0.0).astype(BF16)
        right = jnp.where(col_iota == at_col, mass, 0.0).astype(BF16)
        density[...] += lax.dot_general(
            left, right, (((1,), (1,)), ((), ())), preferred_element_type=F32
        )

    bytes_in(brecv.at[pl.ds(0, 7)], bead_r.at[my_crowd], beside)
    splat(my_crowd)

    def splat_next(i, carry):
        crowd = near_crowd(i)
        bytes_in(brecv.at[pl.ds(0, 8)], bead_r.at[crowd], beside)
        splat(crowd)
        return carry

    lax.fori_loop(1, crowds, splat_next, 0)

    def plane_of(z):
        return jnp.concatenate(
            [density[(c * zn + z) * xn : (c * zn + z + 1) * xn, :] for c in range(yc)], axis=1
        )

    d_own = [blur_y(plane_of(z), "g") for z in range(zn)]
    pack_x(mx1_send, [(d_own[2 * i], d_own[2 * i + 1]) for i in range(zn // 2)])
    start(m_x1)

    t_own = [tgt[i] for i in range(zn)]
    wait_recv(t_z)
    t_g, t_d = blur_z(z_planes(t_own, tz), ("g", "d"))
    pack_x(tx_send, list(zip(t_g, t_d)))
    start(t_x)

    wait_recv(m_x1)
    for i in range(zn // 2):
        halves = unpack_x(mx1_recv[0, i], mx1_recv[1, i])
        for j in range(2):
            left, right = halves[j]
            (m1[2 * i + j],) = blur_x(left, d_own[2 * i + j], right, ("g",))
    start(m_z1)

    wait_recv(m_z1)
    (m_own,) = blur_z(z_planes([m1[i] for i in range(zn)], mz1), ("g",))
    for i in range(zn):
        mfull[i] = m_own[i]
    start(m_z2)

    cross = total_of(sum(m_own[i] * tgt[i] for i in range(zn)))
    m_sq = total_of(sum(m_own[i] * m_own[i] for i in range(zn)))
    t_sq = total_of(sum(tgt[i] * tgt[i] for i in range(zn)))
    lane1 = lax.broadcasted_iota(jnp.int32, (1, 128), 1)
    part = jnp.where(
        lane1 == 0, cross, jnp.where(lane1 == 1, m_sq, jnp.where(lane1 == 2, t_sq, 0.0))
    )
    s1_send[...] = part
    s1_recv[me] = part
    start_bricks(brick_sum_copy)

    wait_recv(m_z2)
    m_g, m_d = blur_z(z_planes([mfull[i] for i in range(zn)], mz2), ("g", "d"))
    pack_x(mx2_send, list(zip(m_g, m_d)))
    start(m_x2)

    bytes_in(s1_recv.at[pl.ds(0, nb - 1)], sum_r.at[0], beside)
    part = jnp.sum(s1_recv[...], axis=0)
    s2_send[...] = part
    s2_recv[my] = part

    def one_relay(i, carry):
        relay_sum_copy(lax.rem(my + i, nr)).start()
        return carry

    lax.fori_loop(1, nr, one_relay, 0)

    bytes_in(lrecv.at[pl.ds(0, (nb - 1) * 8)], lev_r, beside)
    wait_recv(t_x)
    wait_recv(m_x2)
    bytes_in(s2_recv.at[pl.ds(0, nr - 1)], sum_r.at[1], {"relay": r_up})
    sums = jnp.sum(s2_recv[...], axis=0)
    cross, m_sq, t_sq = sums[:, 0:1], sums[:, 1:2], sums[:, 2:3]
    norm_m = jnp.sqrt(m_sq + EPSILON)
    norm_t = jnp.sqrt(t_sq + EPSILON)
    corr = cross / (norm_m * norm_t)
    voxels = float(nb * xn * nr * zn * yn)
    of_target = voxels / (norm_m * norm_t)
    of_model = voxels * corr / (norm_m * norm_m)

    parts = [[], [], []]
    for i in range(zn):
        along = of_target * t_g[i] - of_model * m_g[i]
        across = of_target * t_d[i] - of_model * m_d[i]
        (left_g, right_g), (left_d, right_d) = unpack_x(
            of_target * tx_recv[0, i] - of_model * mx2_recv[0, i],
            of_target * tx_recv[1, i] - of_model * mx2_recv[1, i],
        )
        smooth, slope = blur_x(left_g, along, right_g, ("g", "d"))
        (rest,) = blur_x(left_d, across, right_d, ("g",))
        parts[0].append(blur_y(slope, "g"))
        parts[1].append(blur_y(smooth, "d"))
        parts[2].append(blur_y(rest, "g"))
    for f in range(3):
        stacked = jnp.concatenate(
            [parts[f][z][:, c * WIDE : (c + 1) * WIDE] for c in range(yc) for z in range(zn)],
            axis=0,
        )
        high = stacked.astype(BF16)
        low = (stacked - high.astype(F32)).astype(BF16)
        lhs[pl.ds(f * rows, rows), 0:WIDE] = high
        lhs[pl.ds(f * rows, rows), WIDE : 2 * WIDE] = low

    srow_iota = lax.broadcasted_iota(jnp.int32, (rows, 8 * beads), 0)
    scol_iota = lax.broadcasted_iota(jnp.int32, (WIDE, 8 * beads), 0)
    sub = lax.broadcasted_iota(jnp.int32, (8, beads), 0)
    lane = lax.broadcasted_iota(jnp.int32, (8, 128), 1)

    def sample(crowd):
        rows_out = []
        for h in range(2):
            base = crowd * 8 + h * 4
            pieces = []
            for j in range(4):
                two = brecv[base + j]
                pieces += [two[0:1], two[1:2]]
            code = lax.bitwise_and(jnp.concatenate(pieces, axis=1), 65535)
            at_row = lax.shift_right_logical(code, 8)
            at_col = lax.bitwise_and(code, WIDE - 1)
            hot = jnp.where(scol_iota == at_col, 1.0, 0.0).astype(BF16)
            found = jnp.dot(
                lhs[...], jnp.concatenate([hot, hot], axis=0), preferred_element_type=F32
            )
            here = srow_iota == at_row
            grads = []
            for f in range(3):
                value = jnp.sum(
                    jnp.where(here, found[f * rows : (f + 1) * rows], 0.0),
                    axis=0,
                    keepdims=True,
                )
                tile = jnp.zeros((8, beads), F32)
                for s in range(8):
                    piece = jnp.broadcast_to(value[:, s * beads : (s + 1) * beads], (8, beads))
                    tile = jnp.where(sub == s, piece, tile)
                grads.append(tile)
            gx, gy, gz = grads
            start8 = pl.multiple_of(base * 8, 8)
            mass, ux, uy, uz = [lrecv[pl.ds(start8 + j, 8, stride=4), :] for j in range(4)]
            six = (
                mass * gx,
                mass * gy,
                mass * gz,
                uy * gz - uz * gy,
                uz * gx - ux * gz,
                ux * gy - uy * gx,
            )
            tile = jnp.zeros((8, 128), F32)
            for j, term in enumerate(six):
                tile = jnp.where(lane == j, jnp.sum(term, axis=1, keepdims=True), tile)
            rows_out.append(tile)
        for h in range(2):
            for j in range(4):
                rsend[crowd * 8 + h * 4 + j] = rows_out[h][2 * j : 2 * j + 2]

    def sample_next(i, carry):
        crowd = near_crowd(crowds - 1 - i)
        sample(crowd)
        start_crowd(return_copy, crowd)
        return carry

    lax.fori_loop(0, crowds - 1, sample_next, 0)
    sample(my_crowd)
    start_own(return_copy)
    rrecv[me] = rsend[me]

    for pair in (t_z, t_x, m_x1, m_z1, m_z2, m_x2):
        for copy in pair:
            copy.wait_send()
    bytes_out(bsend.at[pl.ds(0, nb - 1)], bead_s, beside)
    bytes_out(lsend.at[pl.ds(0, (nb - 1) * 8)], lev_s, beside)
    bytes_out(s1_recv.at[pl.ds(0, nb - 1)], sum_s.at[0], beside)
    bytes_out(s2_recv.at[pl.ds(0, nr - 1)], sum_s.at[1], {"relay": r_up})

    def take_in(crowd):
        for j in range(8):
            fin[pl.ds(pl.multiple_of(crowd * 16, 16) + 2 * j, 2), :] = rrecv[crowd * 8 + j]

    def take_next(i, carry):
        crowd = near_crowd(crowds - 1 - i)
        bytes_in(rrecv.at[pl.ds(0, 8)], ret_r.at[crowd], beside)
        take_in(crowd)
        return carry

    lax.fori_loop(0, crowds - 1, take_next, 0)
    bytes_in(rrecv.at[pl.ds(0, 7)], ret_r.at[my_crowd], beside)
    take_in(my_crowd)
    got = fin[...]
    for j in range(6):
        out[pl.ds(j, 1), :] = jnp.sum(picks * got[:, j : j + 1], axis=0, keepdims=True)
    bytes_out(rsend.at[pl.ds(0, nb - 1)], ret_s, beside)


def shards(target, frag_brick, bead_cell, bead_weight, bead_arm, frag_angle):
    nb, nr = lax.axis_size("brick"), lax.axis_size("relay")
    frags, beads = bead_cell.shape
    zn, xn, yn = target.shape
    rows = zn * xn * (yn // WIDE)
    sizes = (nb, nr, frags, beads, zn, xn, yn)
    vmem = pltpu.VMEM
    block = (zn, xn, yn)
    dma = pltpu.SemaphoreType.DMA
    crowds = nb // 8
    scratch = [
        vmem(block, F32),
        vmem((1, frags), jnp.int32),
        vmem((frags, beads), jnp.int32),
        vmem((frags, beads), BF16),
        vmem((3, frags, beads), F32),
        vmem((3, frags), F32),
        vmem((nb, 2, beads), jnp.int32),
        vmem((nb, 2, beads), jnp.int32),
        vmem((nb * 8, beads), F32),
        vmem((nb * 8, beads), F32),
        vmem((nb, 2, 128), F32),
        vmem((nb, 2, 128), F32),
        vmem((2 * nb, 128), F32),
        vmem((2,) + block, F32),
        vmem((2,) + block, F32),
        vmem((2,) + block, F32),
        vmem(block, F32),
        vmem(block, F32),
        vmem((2,) + block, F32),
        vmem((2,) + block, F32),
        vmem((2, zn // 2, xn, yn), F32),
        vmem((2, zn // 2, xn, yn), F32),
        vmem((2,) + block, F32),
        vmem((2,) + block, F32),
        vmem((1, 128), F32),
        vmem((nb, 1, 128), F32),
        vmem((1, 128), F32),
        vmem((nr, 1, 128), F32),
        vmem((rows, WIDE), F32),
        vmem((3 * rows, 2 * WIDE), BF16),
        dma((6,)),
        dma,
        dma((crowds,)),
        dma,
        dma,
        dma,
        dma((crowds,)),
        dma((2,)),
        dma((2,)),
        dma((12,)),
        dma((12,)),
    ]
    away = pl.BlockSpec(memory_space=pl.ANY)
    return pl.pallas_call(
        functools.partial(body, sizes),
        out_shape=jax.ShapeDtypeStruct((6, frags), F32),
        in_specs=[away] * 6,
        out_specs=pl.BlockSpec(memory_space=pltpu.VMEM),
        scratch_shapes=scratch,
        compiler_params=pltpu.CompilerParams(
            collective_id=0, has_side_effects=True, vmem_limit_bytes=56 * 1024 * 1024
        ),
    )(target, frag_brick.reshape(1, frags), bead_cell, bead_weight, bead_arm, frag_angle)


def solution(mesh):
    placed = (
        P("relay", "brick", None),
        P(("brick", "relay"), None),
        P(("brick", "relay"), None),
        P(("brick", "relay"), None),
        P(None, ("brick", "relay"), None),
        P(None, ("brick", "relay")),
    )
    return jax.shard_map(
        shards, mesh=mesh, in_specs=placed, out_specs=P(None, ("brick", "relay")), check_vma=False
    )
```

```python
import functools

import jax
import jax.numpy as jnp
import numpy as np
from jax import lax
from jax.experimental import pallas as pl
from jax.experimental.pallas import tpu as pltpu
from jax.sharding import PartitionSpec as P

KR = 4
SIGMA = 1.5
EPSILON = 1e-06
WIDE = 256
CUTS = 2
F32 = jnp.float32
BF16 = jnp.bfloat16
MESH = pl.DeviceIdType.MESH


def kernel_values(half_width, derivative):
    offsets = np.arange(-half_width, half_width + 1) * 1.0
    gaussian = np.exp(-(offsets**2) / (2.0 * SIGMA**2))
    gaussian = gaussian / gaussian.sum()
    if derivative:
        return -offsets / SIGMA**2 * gaussian
    return gaussian


SMOOTH = [float(v) for v in kernel_values(KR, False)]
SLOPE = [float(v) for v in kernel_values(KR, True)]
STEPS = 32767.0
STEEP = 1.001 * float(-kernel_values(KR, True)[KR + 1 :].sum())
TINY = 1e-30


def to_fixed(value, per_unit):
    steps = jnp.clip(jnp.floor(value * per_unit + 0.5), -STEPS, STEPS)
    return steps.astype(jnp.int32).astype(jnp.int16)


def from_fixed(steps, unit):
    return steps.astype(jnp.int32).astype(F32) * unit


def combine(behind, ahead, centre, which):
    if which == "g":
        total = SMOOTH[KR] * centre
        for t in range(1, KR + 1):
            total = total + SMOOTH[KR + t] * (behind[t - 1] + ahead[t - 1])
        return total
    total = SLOPE[KR + 1] * (behind[0] - ahead[0])
    for t in range(2, KR + 1):
        total = total + SLOPE[KR + t] * (behind[t - 1] - ahead[t - 1])
    return total


def blur_y(plane, which):
    rows, length = plane.shape
    wide = jnp.concatenate([plane, jnp.zeros((rows, 128), F32)], axis=1)
    behind = [pltpu.roll(wide, t, 1)[:, :length] for t in range(1, KR + 1)]
    ahead = [pltpu.roll(wide, length + 128 - t, 1)[:, :length] for t in range(1, KR + 1)]
    return combine(behind, ahead, plane, which)


def blur_x(left, own, right, kinds):
    cols = own.shape[0]
    row = lax.broadcasted_iota(jnp.int32, own.shape, 0)
    behind = [
        pltpu.roll(jnp.where(row >= cols - t, left, own), t, 0) for t in range(1, KR + 1)
    ]
    ahead = [
        pltpu.roll(jnp.where(row < t, right, own), cols - t, 0) for t in range(1, KR + 1)
    ]
    return [combine(behind, ahead, own, kind) for kind in kinds]


def blur_z(planes, kinds):
    own = len(planes) - 2 * KR
    done = []
    for kind in kinds:
        done.append(
            [
                combine(
                    [planes[KR + i - t] for t in range(1, KR + 1)],
                    [planes[KR + i + t] for t in range(1, KR + 1)],
                    planes[KR + i],
                    kind,
                )
                for i in range(own)
            ]
        )
    return done


def swap(plane):
    return pltpu.roll(plane, 4, 0)


def ring_near(j):
    return j + j // 2 - 2 * (j // 3)


def total_of(value):
    return jnp.sum(jnp.sum(value, axis=1, keepdims=True), axis=0, keepdims=True)


def body(
    sizes,
    tgt_in,
    brick_in,
    cell_in,
    weight_in,
    arm_in,
    angle_in,
    out,
    tgt,
    brick_of,
    cell,
    weight,
    arm,
    angle,
    bsend,
    brecv,
    lsend,
    lrecv,
    rsend,
    rrecv,
    fin,
    tz,
    mz1,
    mz2,
    m1,
    mfull,
    q1,
    q2,
    unit_send,
    unit_recv,
    tx_send,
    tx_recv,
    mx1_send,
    mx1_recv,
    mx2_send,
    mx2_recv,
    s1_send,
    s1_recv,
    s2_send,
    s2_recv,
    density,
    t_fields,
    m_fields,
    lhs,
    lhs_m,
    t_sums,
    load,
    bead_s,
    bead_r,
    lev_s,
    lev_r,
    ret_s,
    ret_r,
    sum_s,
    sum_r,
    halo_s,
    halo_r,
    unit_s,
    unit_r,
):
    nb, nr, frags, beads, zn, xn, yn = sizes
    yc = yn // WIDE
    rows = zn * xn * yc
    slots = 2 * nb
    crowds = nb // 8
    wide_x = crowds // 2
    me = lax.axis_index("brick")
    my = lax.axis_index("relay")
    my_crowd = me // 8
    my_x, my_half = my_crowd // 2, my_crowd % 2
    b_up, b_down = lax.rem(me + 1, nb), lax.rem(me + nb - 1, nb)
    r_up, r_down = lax.rem(my + 1, nr), lax.rem(my + nr - 1, nr)
    has_left = jnp.where(me > 0, 1.0, 0.0).astype(F32)
    has_right = jnp.where(me < nb - 1, 1.0, 0.0).astype(F32)
    has_low = jnp.where(my > 0, 1.0, 0.0).astype(F32)
    has_high = jnp.where(my < nr - 1, 1.0, 0.0).astype(F32)

    def near_crowd(i):
        return lax.rem(my_x + ring_near(i // 2), wide_x) * 2 + lax.rem(my_half + i % 2, 2)

    barrier = pltpu.get_barrier_semaphore()

    loads = [
        pltpu.make_async_copy(src, dst, load.at[i])
        for i, (src, dst) in enumerate(
            (
                (brick_in, brick_of),
                (cell_in, cell),
                (weight_in, weight),
                (tgt_in, tgt),
                (arm_in, arm),
                (angle_in, angle),
            )
        )
    ]
    for copy in loads:
        copy.start()

    def greet(where):
        pl.semaphore_signal(barrier, inc=1, device_id=where, device_id_type=MESH)

    def greet_crowd(i, carry):
        crowd = near_crowd(crowds - i)
        for j in range(8):
            greet({"brick": crowd * 8 + j})
        return carry

    def greet_relay(i, carry):
        greet({"relay": lax.rem(my + i, nr)})
        return carry

    lax.fori_loop(1, crowds, greet_crowd, 0)
    for j in range(1, 8):
        greet({"brick": my_crowd * 8 + lax.rem(me + j, 8)})
    lax.fori_loop(1, nr, greet_relay, 0)
    for copy in loads[:3]:
        copy.wait()

    row_f = lax.broadcasted_iota(jnp.int32, (frags, frags), 0)
    col_f = lax.broadcasted_iota(jnp.int32, (frags, frags), 1)
    brick_row = brick_of[...].astype(F32)
    brick_col = jnp.sum(jnp.where(row_f == col_f, brick_row, 0.0), axis=1, keepdims=True)
    twin = jnp.where((brick_col == brick_row) & (row_f < col_f), 1.0, 0.0)
    rank_row = jnp.minimum(jnp.sum(twin, axis=0, keepdims=True), 1.0)
    slot_iota = lax.broadcasted_iota(jnp.int32, (slots, frags), 0).astype(F32)
    picks = jnp.where(slot_iota == brick_row * 2.0 + rank_row, 1.0, 0.0)

    cells = cell[...].astype(F32)
    line = jnp.floor((cells + 0.5) * (1.0 / yn))
    y_pos = cells - line * yn
    chunk = jnp.floor((y_pos + 0.5) * (1.0 / WIDE))
    column = y_pos - chunk * WIDE
    row_id = chunk * (zn * xn) + line
    w = weight[...]
    w32 = w.astype(F32)
    early = jnp.concatenate([row_id.astype(BF16), column.astype(BF16), w], axis=1)
    sent = jnp.dot(picks.astype(BF16), early, preferred_element_type=F32)
    code = (sent[:, :beads] * WIDE + sent[:, beads : 2 * beads]).astype(jnp.int32)
    packed = (sent[:, 2 * beads :] * 512.0).astype(jnp.int32) * 65536 + code
    for p in range(nb):
        bsend[p] = packed[2 * p : 2 * p + 2]

    pl.semaphore_wait(barrier, nb + nr - 2)

    def bead_copy(far):
        return pltpu.make_async_remote_copy(
            src_ref=bsend.at[far],
            dst_ref=brecv.at[me],
            send_sem=bead_s,
            recv_sem=bead_r.at[my_crowd],
            device_id={"brick": far},
            device_id_type=MESH,
        )

    def lever_copy(far):
        return pltpu.make_async_remote_copy(
            src_ref=lsend.at[pl.ds(pl.multiple_of(far * 8, 8), 8)],
            dst_ref=lrecv.at[pl.ds(pl.multiple_of(me * 8, 8), 8)],
            send_sem=lev_s,
            recv_sem=lev_r,
            device_id={"brick": far},
            device_id_type=MESH,
        )

    def return_copy(far):
        return pltpu.make_async_remote_copy(
            src_ref=rsend.at[far],
            dst_ref=rrecv.at[me],
            send_sem=ret_s,
            recv_sem=ret_r.at[my_crowd],
            device_id={"brick": far},
            device_id_type=MESH,
        )

    def brick_sum_copy(far):
        return pltpu.make_async_remote_copy(
            src_ref=s1_send,
            dst_ref=s1_recv.at[me],
            send_sem=sum_s.at[0],
            recv_sem=sum_r.at[0],
            device_id={"brick": far},
            device_id_type=MESH,
        )

    def relay_sum_copy(far):
        return pltpu.make_async_remote_copy(
            src_ref=s2_send,
            dst_ref=s2_recv.at[my],
            send_sem=sum_s.at[1],
            recv_sem=sum_r.at[1],
            device_id={"relay": far},
            device_id_type=MESH,
        )

    def bytes_in(ref, sem, where):
        pltpu.make_async_remote_copy(
            src_ref=ref,
            dst_ref=ref,
            send_sem=sem,
            recv_sem=sem,
            device_id=where,
            device_id_type=MESH,
        ).wait_recv()

    def bytes_out(ref, sem, where):
        pltpu.make_async_remote_copy(
            src_ref=ref,
            dst_ref=ref,
            send_sem=sem,
            recv_sem=sem,
            device_id=where,
            device_id_type=MESH,
        ).wait_send()

    beside = {"brick": b_up}

    def start_crowd(copy, crowd):
        for j in range(8):
            copy(crowd * 8 + j).start()

    def start_own(copy):
        for j in range(1, 8):
            copy(my_crowd * 8 + lax.rem(me + j, 8)).start()

    def start_bricks(copy):
        def one(i, carry):
            start_crowd(copy, near_crowd(crowds - 1 - i))
            return carry

        lax.fori_loop(0, crowds - 1, one, 0)
        start_own(copy)

    def start_near(copy):
        def one(i, carry):
            start_crowd(copy, near_crowd(i))
            return carry

        start_own(copy)
        lax.fori_loop(1, crowds, one, 0)

    def exchange(below, above, got, send_sem, recv_sem, axis):
        up, down = (b_up, b_down) if axis == "brick" else (r_up, r_down)
        for src, dst, far in ((above, got.at[0], up), (below, got.at[1], down)):
            pltpu.make_async_remote_copy(
                src_ref=src,
                dst_ref=dst,
                send_sem=send_sem,
                recv_sem=recv_sem,
                device_id={axis: far},
                device_id_type=MESH,
            ).start()

    def z_planes(own, got):
        return (
            [got[0, i] * has_low for i in range(zn)]
            + own
            + [got[1, i] * has_high for i in range(zn)]
        )

    def z_fixed(own, got, low, high):
        sides = []
        for d, unit in ((0, low * has_low), (1, high * has_high)):
            both = [from_fixed(got[d, j], unit) for j in range(zn // 2)]
            sides.append([half[k * xn : (k + 1) * xn] for half in both for k in range(2)])
        return sides[0] + own + sides[1]

    def put_fixed(dst, planes, per_unit):
        for j in range(zn // 2):
            pair = jnp.concatenate([planes[2 * j], planes[2 * j + 1]], axis=0)
            dst[j] = to_fixed(pair, per_unit)

    def send_unit(number, unit, axis):
        unit_send[number] = jnp.broadcast_to(unit, (1, 128))
        exchange(
            unit_send.at[number],
            unit_send.at[number],
            unit_recv.at[number],
            unit_s.at[number],
            unit_r.at[number],
            axis,
        )

    def get_units(number):
        bytes_in(unit_recv.at[number], unit_r.at[number], beside)
        return unit_recv[number, 0, :, 0:1], unit_recv[number, 1, :, 0:1]

    def pack_edges(one, two):
        row = lax.broadcasted_iota(jnp.int32, one.shape, 0)
        return jnp.where(row < 4, swap(one), two), jnp.where(row < 4, one, swap(two))

    def pack_x(send, pairs):
        for i, (one, two) in enumerate(pairs):
            send[0, i], send[1, i] = pack_edges(one, two)

    def unpack_x(from_left, from_right):
        from_left, from_right = from_left * has_left, from_right * has_right
        return (swap(from_left), from_right), (from_left, swap(from_right))

    start_near(bead_copy)
    brecv[me] = bsend[me]
    for copy in loads[3:]:
        copy.wait()
    exchange(tgt, tgt, tz, halo_s.at[0], halo_r.at[0], "relay")

    cos_sin = []
    for j in range(3):
        turn = angle[pl.ds(j, 1), :]
        pair = []
        for fn in (jnp.cos, jnp.sin):
            pair.append(
                jnp.sum(jnp.where(row_f == col_f, fn(turn), 0.0), axis=1, keepdims=True)
            )
        cos_sin.append(pair)
    (cos_a, sin_a), (cos_b, sin_b), (cos_c, sin_c) = cos_sin
    rot = [
        [
            cos_a * cos_b,
            cos_a * sin_b * sin_c - sin_a * cos_c,
            cos_a * sin_b * cos_c + sin_a * sin_c,
        ],
        [
            sin_a * cos_b,
            sin_a * sin_b * sin_c + cos_a * cos_c,
            sin_a * sin_b * cos_c - cos_a * sin_c,
        ],
        [-sin_b, cos_b * sin_c, cos_b * cos_c],
    ]
    arms = [arm[j] for j in range(3)]
    late = [w32]
    for j in range(3):
        late.append(w32 * (rot[j][0] * arms[0] + rot[j][1] * arms[1] + rot[j][2] * arms[2]))
    late = jnp.concatenate(late, axis=1)
    moved = jnp.dot(
        picks, late, precision=lax.Precision.HIGHEST, preferred_element_type=F32
    )
    for j in range(4):
        lsend[pl.ds(j, slots, stride=4), :] = moved[:, j * beads : (j + 1) * beads]

    start_near(lever_copy)
    mine8 = pl.ds(pl.multiple_of(me * 8, 8), 8)
    lrecv[mine8, :] = lsend[mine8, :]

    scol_iota = lax.broadcasted_iota(jnp.int32, (WIDE, 8 * beads), 0)
    ssub_iota = lax.broadcasted_iota(jnp.int32, (8, 8 * beads), 0)
    sub = lax.broadcasted_iota(jnp.int32, (8, beads), 0)
    lane = lax.broadcasted_iota(jnp.int32, (8, 128), 1)

    def put_fields(lhs, planes):
        for f in range(3):
            stacked = jnp.concatenate(
                [planes[f, z, :, c * WIDE : (c + 1) * WIDE] for c in range(yc) for z in range(zn)],
                axis=0,
            )
            high = stacked.astype(BF16)
            low = (stacked - high.astype(F32)).astype(BF16)
            lhs[pl.ds(f * rows, rows), :] = high
            lhs[pl.ds((3 + f) * rows, rows), :] = low

    def sample(lhs, quad, tile, first):
        base = quad * 4
        pieces = []
        for j in range(4):
            two = brecv[base + j]
            pieces += [two[0:1], two[1:2]]
        code = lax.bitwise_and(jnp.concatenate(pieces, axis=1), 65535)
        at_col = lax.bitwise_and(code, WIDE - 1)
        at_row = lax.shift_right_logical(code, 8)
        group = jnp.broadcast_to(lax.shift_right_logical(at_row, 3), ssub_iota.shape)
        here = ssub_iota == lax.bitwise_and(at_row, 7)
        hot = jnp.where(scol_iota == at_col, 1.0, 0.0).astype(BF16)
        found = jnp.dot(lhs[...], hot, preferred_element_type=F32)
        picked = [found[f * rows : f * rows + 8] for f in range(6)]
        for g in range(1, rows // 8):
            match = group == g
            for f in range(6):
                at = f * rows + g * 8
                picked[f] = jnp.where(match, found[at : at + 8], picked[f])
        grads = []
        for f in range(3):
            value = jnp.sum(
                jnp.where(here, picked[f] + picked[3 + f], 0.0), axis=0, keepdims=True
            )
            whole = jnp.zeros((8, beads), F32)
            for s in range(8):
                piece = jnp.broadcast_to(value[:, s * beads : (s + 1) * beads], (8, beads))
                whole = jnp.where(sub == s, piece, whole)
            grads.append(whole)
        gx, gy, gz = grads
        start8 = pl.multiple_of(base * 8, 8)
        mass, ux, uy, uz = [lrecv[pl.ds(start8 + j, 8, stride=4), :] for j in range(4)]
        six = (
            mass * gx,
            mass * gy,
            mass * gz,
            uy * gz - uz * gy,
            uz * gx - ux * gz,
            ux * gy - uy * gx,
        )
        for j, term in enumerate(six):
            tile = jnp.where(lane == first + j, jnp.sum(term, axis=1, keepdims=True), tile)
        return tile

    ahead = max(1, crowds // 4)

    def sample_target(i, carry):
        crowd = near_crowd(crowds - 1 - i)
        quads = [crowd * 2, crowd * 2 + 1]
        tiles = [sample(lhs, quad, jnp.zeros((8, 128), F32), 0) for quad in quads]
        for quad, tile in zip(quads, tiles):
            t_sums[quad] = tile
        return carry

    def to_send(quads, tiles):
        for quad, tile in zip(quads, tiles):
            for j in range(4):
                rsend[quad * 4 + j] = tile[2 * j : 2 * j + 2]

    def sample_model(i, carry):
        crowd = near_crowd(crowds - 1 - i)
        quads = [crowd * 2, crowd * 2 + 1]
        to_send(quads, [sample(lhs_m, quad, t_sums[quad], 6) for quad in quads])
        start_crowd(return_copy, crowd)
        return carry

    def sample_both(quads):
        to_send(quads, [sample(lhs, quad, jnp.zeros((8, 128), F32), 0) for quad in quads])

    def sample_next(i, carry):
        crowd = near_crowd(crowds - 1 - i)
        sample_both([crowd * 2, crowd * 2 + 1])
        start_crowd(return_copy, crowd)
        return carry

    row_iota = lax.broadcasted_iota(jnp.int32, (rows, 32 * beads), 0)
    col_iota = lax.broadcasted_iota(jnp.int32, (WIDE, 32 * beads), 0)
    density[...] = jnp.zeros_like(density)

    def splat(pair):
        pieces = []
        for j in range(16):
            two = brecv[pair * 16 + j]
            pieces += [two[0:1], two[1:2]]
        word = jnp.concatenate(pieces, axis=1)
        code = lax.bitwise_and(word, 65535)
        mass = lax.shift_right_logical(word, 16).astype(F32) * (1.0 / 512.0)
        at_row = lax.shift_right_logical(code, 8)
        at_col = lax.bitwise_and(code, WIDE - 1)
        left = jnp.where(row_iota == at_row, 1.0, 0.0).astype(BF16)
        right = jnp.where(col_iota == at_col, mass, 0.0).astype(BF16)
        density[...] += lax.dot_general(
            left, right, (((1,), (1,)), ((), ())), preferred_element_type=F32
        )

    bytes_in(brecv.at[pl.ds(0, 7)], bead_r.at[my_crowd], beside)
    bytes_in(brecv.at[pl.ds(0, 8)], bead_r.at[near_crowd(1)], beside)
    splat(my_x)

    def splat_next(i, carry):
        for j in range(2):
            bytes_in(brecv.at[pl.ds(0, 8)], bead_r.at[near_crowd(2 * i + j)], beside)
        splat(near_crowd(2 * i) // 2)
        return carry

    half = max(1, wide_x - 1)
    lax.fori_loop(1, half, splat_next, 0)

    t_own = [tgt[i] for i in range(zn)]
    bytes_in(tz, halo_r.at[0], beside)
    t_g, t_d = blur_z(z_planes(t_own, tz), ("g", "d"))
    pack_x(tx_send, list(zip(t_g, t_d)))
    exchange(tx_send.at[1], tx_send.at[0], tx_recv, halo_s.at[1], halo_r.at[1], "brick")

    lax.fori_loop(half, wide_x, splat_next, 0)

    def plane_of(z):
        return jnp.concatenate(
            [density[(c * zn + z) * xn : (c * zn + z + 1) * xn, :] for c in range(yc)], axis=1
        )

    cut = yn // CUTS

    def piece(plane, c):
        return plane[:, c * cut : (c + 1) * cut]

    def peak_of(planes):
        top = planes[0]
        for plane in planes[1:]:
            top = jnp.maximum(top, plane)
        top = jnp.max(jnp.max(top, axis=0, keepdims=True), axis=1, keepdims=True)
        return jnp.maximum(top, TINY)

    d_own = [blur_y(plane_of(z), "g") for z in range(zn)]
    peak = peak_of(d_own)
    send_unit(3, peak * (1.0 / STEPS), "brick")
    for c in range(CUTS):
        d_cut = [piece(plane, c) for plane in d_own]
        edges = [pack_edges(d_cut[2 * i], d_cut[2 * i + 1]) for i in range(zn // 2)]
        for d in range(2):
            for j in range(zn // 4):
                pair = jnp.concatenate([edges[2 * j][d], edges[2 * j + 1][d]], axis=0)
                mx1_send[c, d, j] = to_fixed(pair, STEPS / peak)
        exchange(
            mx1_send.at[c, 1], mx1_send.at[c, 0], mx1_recv.at[c], halo_s.at[2], halo_r.at[2 + c], "brick"
        )

    def gradients(along, across, left, right):
        (left_g, right_g), (left_d, right_d) = unpack_x(left, right)
        smooth, slope = blur_x(left_g, along, right_g, ("g", "d"))
        (rest,) = blur_x(left_d, across, right_d, ("g",))
        return slope, smooth, rest

    base = 2 + CUTS
    from_left, from_right = get_units(3)
    for c in range(CUTS):
        bytes_in(mx1_recv.at[c], halo_r.at[2 + c], beside)
        sides = []
        for d, unit in ((0, from_left), (1, from_right)):
            both = [from_fixed(mx1_recv[c, d, j], unit) for j in range(zn // 4)]
            sides.append([half[k * xn : (k + 1) * xn] for half in both for k in range(2)])
        for i in range(zn // 2):
            halves = unpack_x(sides[0][i], sides[1][i])
            for j in range(2):
                left, right = halves[j]
                (m1[c, 2 * i + j],) = blur_x(left, piece(d_own[2 * i + j], c), right, ("g",))
    peak = jnp.maximum(peak, jnp.maximum(from_left, from_right) * STEPS)
    send_unit(0, peak * (1.0 / STEPS), "relay")
    for c in range(CUTS):
        put_fixed(q1.at[c], [m1[c, i] for i in range(zn)], STEPS / peak)
        exchange(q1.at[c], q1.at[c], mz1.at[c], halo_s.at[3], halo_r.at[base + c], "relay")

    bytes_in(tx_recv, halo_r.at[1], beside)
    kinds = ("g", "d", "g")
    t_sq = total_of(sum(tgt[i] * tgt[i] for i in range(zn)))
    for i in range(zn):
        parts = gradients(t_g[i], t_d[i], tx_recv[0, i], tx_recv[1, i])
        for f in range(3):
            t_fields[f, i] = blur_y(parts[f], kinds[f])
    put_fields(lhs, t_fields)
    bytes_in(lrecv.at[pl.ds(0, (nb - 1) * 8)], lev_r, beside)
    lax.fori_loop(0, 1, sample_target, 0)


    base += CUTS
    cross, m_sq = 0.0, 0.0
    low, high = get_units(0)
    peak = jnp.maximum(peak, jnp.maximum(low, high) * STEPS)
    send_unit(1, peak * (1.0 / STEPS), "relay")
    for c in range(CUTS):
        bytes_in(mz1.at[c], halo_r.at[base - CUTS + c], beside)
        (m_own,) = blur_z(z_fixed([m1[c, i] for i in range(zn)], mz1.at[c], low, high), ("g",))
        for i in range(zn):
            mfull[c, i] = m_own[i]
        put_fixed(q2.at[c], m_own, STEPS / peak)
        exchange(q2.at[c], q2.at[c], mz2.at[c], halo_s.at[4], halo_r.at[base + c], "relay")
        cross = cross + sum(m_own[i] * piece(tgt[i], c) for i in range(zn))
        m_sq = m_sq + sum(m_own[i] * m_own[i] for i in range(zn))
    cross, m_sq = total_of(cross), total_of(m_sq)
    lane1 = lax.broadcasted_iota(jnp.int32, (1, 128), 1)
    part = jnp.where(
        lane1 == 0, cross, jnp.where(lane1 == 1, m_sq, jnp.where(lane1 == 2, t_sq, 0.0))
    )
    s1_send[...] = part
    s1_recv[me] = part
    start_bricks(brick_sum_copy)
    lax.fori_loop(1, ahead, sample_target, 0)

    base += CUTS
    m_g, m_d = [], []
    low, high = get_units(1)
    peak = jnp.maximum(peak, jnp.maximum(low, high) * STEPS)
    send_unit(2, peak * (1.0 / STEPS), "brick")
    for c in range(CUTS):
        bytes_in(mz2.at[c], halo_r.at[base - CUTS + c], beside)
        along, across = blur_z(
            z_fixed([mfull[c, i] for i in range(zn)], mz2.at[c], low, high), ("g", "d")
        )
        m_g.append(along)
        m_d.append(across)
        edges = [
            pack_edges(one * (STEPS / peak), two * (STEPS / (STEEP * peak)))
            for one, two in zip(along, across)
        ]
        for d in range(2):
            put_fixed(mx2_send.at[c, d], [edge[d] for edge in edges], 1.0)
        exchange(
            mx2_send.at[c, 1], mx2_send.at[c, 0], mx2_recv.at[c], halo_s.at[5], halo_r.at[base + c], "brick"
        )

    from_left, from_right = get_units(2)
    cuts = [[[], [], []] for i in range(zn)]
    for c in range(CUTS):
        bytes_in(mx2_recv.at[c], halo_r.at[base + c], beside)
        sides = []
        for d, unit in ((0, from_left), (1, from_right)):
            row = lax.broadcasted_iota(jnp.int32, (xn, cut), 0)
            units = jnp.where(row < 4, unit, unit * STEEP)
            both = [from_fixed(mx2_recv[c, d, j], 1.0) for j in range(zn // 2)]
            sides.append([half[k * xn : (k + 1) * xn] * units for half in both for k in range(2)])
        for i in range(zn):
            got = gradients(m_g[c][i], m_d[c][i], sides[0][i], sides[1][i])
            for f in range(3):
                cuts[i][f].append(got[f])
    bytes_in(s1_recv.at[pl.ds(0, nb - 1)], sum_r.at[0], beside)
    part = jnp.sum(s1_recv[...], axis=0)
    s2_send[...] = part
    s2_recv[my] = part

    def one_relay(i, carry):
        relay_sum_copy(lax.rem(my + i, nr)).start()
        return carry

    lax.fori_loop(1, nr, one_relay, 0)

    for f in range(3):
        for i in range(zn):
            m_fields[f, i] = blur_y(jnp.concatenate(cuts[i][f], axis=1), kinds[f])
    put_fields(lhs_m, m_fields)

    lax.fori_loop(0, ahead, sample_model, 0)

    bytes_in(s2_recv.at[pl.ds(0, nr - 1)], sum_r.at[1], {"relay": r_up})
    sums = jnp.sum(s2_recv[...], axis=0)
    cross, m_sq, t_sq = sums[:, 0:1], sums[:, 1:2], sums[:, 2:3]
    norm_m = jnp.sqrt(m_sq + EPSILON)
    norm_t = jnp.sqrt(t_sq + EPSILON)
    corr = cross / (norm_m * norm_t)
    voxels = float(nb * xn * nr * zn * yn)
    of_target = voxels / (norm_m * norm_t)
    of_model = voxels * corr / (norm_m * norm_m)


    ratio = of_model / of_target
    for f in range(3):
        for i in range(zn):
            t_fields[f, i] = t_fields[f, i] - ratio * m_fields[f, i]
    put_fields(lhs, t_fields)
    lax.fori_loop(ahead, crowds - 1, sample_next, 0)
    my_quad = me // 4
    other_quad = my_crowd * 2 + lax.rem(my_quad + 1, 2)
    sample_both([other_quad])
    for j in range(4):
        return_copy(other_quad * 4 + j).start()
    sample_both([my_quad])
    for j in range(1, 4):
        return_copy(my_quad * 4 + lax.rem(me + j, 4)).start()
    rrecv[me] = rsend[me]

    for i, ref in enumerate((tz, tx_send, mx1_send, mz1, mz2, mx2_send)):
        bytes_out(ref, halo_s.at[i], beside)
    for i in range(4):
        bytes_out(unit_recv.at[i], unit_s.at[i], beside)
    bytes_out(bsend.at[pl.ds(0, nb - 1)], bead_s, beside)
    bytes_out(lsend.at[pl.ds(0, (nb - 1) * 8)], lev_s, beside)
    bytes_out(s1_recv.at[pl.ds(0, nb - 1)], sum_s.at[0], beside)
    bytes_out(s2_recv.at[pl.ds(0, nr - 1)], sum_s.at[1], {"relay": r_up})

    def take_in(crowd):
        for j in range(8):
            fin[pl.ds(pl.multiple_of(crowd * 16, 16) + 2 * j, 2), :] = rrecv[crowd * 8 + j]

    def take_next(i, carry):
        crowd = near_crowd(crowds - 1 - i)
        bytes_in(rrecv.at[pl.ds(0, 8)], ret_r.at[crowd], beside)
        take_in(crowd)
        return carry

    lax.fori_loop(0, crowds - 1, take_next, 0)
    bytes_in(rrecv.at[pl.ds(0, 7)], ret_r.at[my_crowd], beside)
    take_in(my_crowd)
    got = fin[...]
    got = of_target * got - of_model * pltpu.roll(got, 128 - 6, 1)
    for j in range(6):
        out[pl.ds(j, 1), :] = jnp.sum(picks * got[:, j : j + 1], axis=0, keepdims=True)
    bytes_out(rsend.at[pl.ds(0, nb - 1)], ret_s, beside)


def shards(target, frag_brick, bead_cell, bead_weight, bead_arm, frag_angle):
    nb, nr = lax.axis_size("brick"), lax.axis_size("relay")
    frags, beads = bead_cell.shape
    zn, xn, yn = target.shape
    rows = zn * xn * (yn // WIDE)
    sizes = (nb, nr, frags, beads, zn, xn, yn)
    vmem = pltpu.VMEM
    block = (zn, xn, yn)
    cut = yn // CUTS
    part = (zn, xn, cut)
    fixed = (zn // 2, 2 * xn, cut)
    dma = pltpu.SemaphoreType.DMA
    crowds = nb // 8
    scratch = [
        vmem(block, F32),
        vmem((1, frags), jnp.int32),
        vmem((frags, beads), jnp.int32),
        vmem((frags, beads), BF16),
        vmem((3, frags, beads), F32),
        vmem((3, frags), F32),
        vmem((nb, 2, beads), jnp.int32),
        vmem((nb, 2, beads), jnp.int32),
        vmem((nb * 8, beads), F32),
        vmem((nb * 8, beads), F32),
        vmem((nb, 2, 128), F32),
        vmem((nb, 2, 128), F32),
        vmem((2 * nb, 128), F32),
        vmem((2,) + block, F32),
        vmem((CUTS, 2) + fixed, jnp.int16),
        vmem((CUTS, 2) + fixed, jnp.int16),
        vmem((CUTS,) + part, F32),
        vmem((CUTS,) + part, F32),
        vmem((CUTS,) + fixed, jnp.int16),
        vmem((CUTS,) + fixed, jnp.int16),
        vmem((4, 1, 128), F32),
        vmem((4, 2, 1, 128), F32),
        vmem((2,) + block, F32),
        vmem((2,) + block, F32),
        vmem((CUTS, 2, zn // 4, 2 * xn, cut), jnp.int16),
        vmem((CUTS, 2, zn // 4, 2 * xn, cut), jnp.int16),
        vmem((CUTS, 2) + fixed, jnp.int16),
        vmem((CUTS, 2) + fixed, jnp.int16),
        vmem((1, 128), F32),
        vmem((nb, 1, 128), F32),
        vmem((1, 128), F32),
        vmem((nr, 1, 128), F32),
        vmem((rows, WIDE), F32),
        vmem((3,) + block, F32),
        vmem((3,) + block, F32),
        vmem((6 * rows, WIDE), BF16),
        vmem((6 * rows, WIDE), BF16),
        vmem((nb // 4, 8, 128), F32),
        dma((6,)),
        dma,
        dma((crowds,)),
        dma,
        dma,
        dma,
        dma((crowds,)),
        dma((2,)),
        dma((2,)),
        dma((6,)),
        dma((2 + 4 * CUTS,)),
        dma((4,)),
        dma((4,)),
    ]
    away = pl.BlockSpec(memory_space=pl.ANY)
    return pl.pallas_call(
        functools.partial(body, sizes),
        out_shape=jax.ShapeDtypeStruct((6, frags), F32),
        in_specs=[away] * 6,
        out_specs=pl.BlockSpec(memory_space=pltpu.VMEM),
        scratch_shapes=scratch,
        compiler_params=pltpu.CompilerParams(
            collective_id=0, has_side_effects=True, vmem_limit_bytes=56 * 1024 * 1024
        ),
    )(target, frag_brick.reshape(1, frags), bead_cell, bead_weight, bead_arm, frag_angle)


def solution(mesh):
    placed = (
        P("relay", "brick", None),
        P(("brick", "relay"), None),
        P(("brick", "relay"), None),
        P(("brick", "relay"), None),
        P(None, ("brick", "relay"), None),
        P(None, ("brick", "relay")),
    )
    return jax.shard_map(
        shards, mesh=mesh, in_specs=placed, out_specs=P(None, ("brick", "relay")), check_vma=False
    )
```
